256 devices in a mesh: row: 4 (over x_lo, core), col: 64 (over y, x_hi, z).
Axes of the slice: x: 4 (x_hi: 2, x_lo: 2; x = x_hi * 2 + x_lo), y: 4, z: 8, core: 2. Of those that a mesh axis runs over, the one named last changes fastest.
Arguments:
- test_points: float32 [3, 4096], P(None, ('row', 'col')), may hold values from 0 to 1
- src_points: float32 [3, 262144], P(None, ('row', 'col')), may hold values from 0 to 1
- currents: float32 [2, 262144], P(None, ('row', 'col')), may hold values from -6 to 6
- near_blocks: float32 [16384, 2, 16, 128], P(('row', 'col')), may hold values from -0.3 to 0.3
- near_dest: int32 [16384, 1], P(('row', 'col')), may hold values from 0 to 63; in each aligned block of 64 rows (0 to 63, 64 to 127, ...) at most 2 rows name the same one
- near_tile: int32 [16384, 1], P(('row', 'col')), may hold values from 0 to 7
Outputs:
- field: float32 [2, 4096], P(None, ('row', 'col'))
The draws below stay inside these ranges and needn't reach their ends.
Inputs may be any that keep to these rules, and one draw needn't show every extreme that they name: `near_dest`: among the 64 blocks held by one device, at most 2 name the same column index; some device reaches 2 in every draw.
All inputs are finite; a program needn't handle non-finite values.
Results may differ from the reference program's by a relative error of at most 0.0003.
Values sent between devices are 32-bit elements; how exact they have to be, the bound alone decides.
A program may use at most 64 MiB of HBM per device.

```python
import math
import jax
import jax.numpy as jnp
import numpy as np
from jax import lax

ROW_DEV = 16
STILE = 128
CAP = 2
ROWS = 4096
SOURCES = 262144
TILES = 8
NEAR_DEV = 64
NEAR_ALL = 16384
N_COL = 64
DEVICES = 256


def place_ends(drawn, rng, low, high):
    dims = drawn.shape
    spot = [jax.random.randint(jax.random.fold_in(rng, axis), (), 0, dims[axis]) for axis in range(len(dims))]
    drawn = drawn.at[tuple(spot)].set(low)
    longest = dims.index(max(dims))
    spot[longest] = (spot[longest] + 1) % dims[longest]
    return drawn.at[tuple(spot)].set(high)


def level_of(own_key, extent, cuts, least, largest):
    gain = 1.0
    for dim, blocks in cuts:
        heights = jax.random.uniform(jax.random.fold_in(jax.random.fold_in(own_key, 6), dim), (blocks,), jnp.float32, least / len(cuts), largest / len(cuts))
        gain = gain * jnp.repeat(jnp.exp(heights), extent[dim] // blocks).reshape((-1,) + (1,) * (len(extent) - 1 - dim))
    return gain


def deal_out(key, own, number, rows, amount, top, reach, lean):
    sequence = jax.random.permutation(key, amount)
    heavy_load, common = portions_of(amount, rows * top, reach, lean, True), portions_of(amount, rows * top, reach, lean, False)
    places = jnp.arange(amount)

    def named(sizes, offset_by):
        used = int((sizes > 0).sum())
        fixed = max(1, used // 4)
        passed = fixed + (places - fixed + offset_by * (used - fixed)) % max(1, amount - fixed)
        return jnp.zeros((amount,), jnp.int32).at[sequence[jnp.where(places < fixed, places, passed)]].set(jnp.asarray(sizes, jnp.int32))

    sizes = jnp.where(number % 4 == 0, named(heavy_load, number // 4), named(common, number - number // 4 - 1))
    mixed = jax.random.permutation(jax.random.fold_in(own, 3), amount)
    source_of, sink = mixed[0:amount // 2 * 2:2], mixed[1:amount // 2 * 2:2]
    slack = jnp.minimum(sizes[source_of] - 1, reach - sizes[sink]) // 2
    slack = jnp.where((source_of == sequence[0]) | (sink == sequence[0]) | (sizes[sink] == 0), 0, jnp.maximum(slack, 0))
    passed = jax.random.randint(jax.random.fold_in(own, 4), (amount // 2,), 0, 1 << 20) % (slack + 1)
    sizes = sizes.at[source_of].add(-passed).at[sink].add(passed)
    items = jnp.searchsorted(jnp.cumsum(sizes), jnp.arange(rows * top), side="right").astype(jnp.int32)
    listing = items.reshape(top, rows).T
    listing = listing[jax.random.permutation(jax.random.fold_in(own, 1), rows)]
    offset_by = jax.random.randint(jax.random.fold_in(own, 2), (rows, 1), 0, top)
    return jnp.take_along_axis(listing, (jnp.arange(top)[None, :] + offset_by) % top, axis=1)


def portions_of(amount, total, most, lean, full):
    weights = [(1 << 20) // math.isqrt(standing ** lean) + 1 for standing in range(1, amount + 1)]
    largest = most if full else min(most, max(-(-total // amount), total * weights[0] // sum(weights)))
    least = 1 if total - largest >= amount - 1 else 0
    given, spare = [largest] + [least] * (amount - 1), total - largest - least * (amount - 1)
    while spare > 0:
        candidates = [i for i in range(1, amount) if given[i] < largest] or [i for i in range(1, amount) if given[i] < most]
        whole, remaining = sum([weights[i] for i in candidates]), spare
        for i in candidates:
            addition = min(most - given[i], max(1, remaining * weights[i] // whole), spare)
            given[i] = given[i] + addition
            spare = spare - addition
    return np.array(given)


def scatter_about(rng, dims, width, reach, cuts=(), held_as=jnp.bfloat16):
    result = jax.random.normal(rng, dims, jnp.float32) * width
    if len(cuts) > 0:
        result = level_of(rng, dims, cuts, -0.22, 0.18) * result
    return jnp.clip(result, min=-reach, max=reach).astype(held_as)


def setup_inputs(seed: int = 0) -> dict:
    arg_keys = jax.random.split(jax.random.key(seed), 7)
    test_points = jnp.clip(1.0 * jax.random.uniform(arg_keys[0], (3, ROWS), jnp.float32) ** level_of(arg_keys[0], (3, ROWS), ((1, 256),), -0.2, 0.2), 0.0, 1.0)
    src_points = jnp.clip(1.0 * jax.random.uniform(arg_keys[1], (3, SOURCES), jnp.float32) ** level_of(arg_keys[1], (3, SOURCES), ((1, 256),), -0.2, 0.2), 0.0, 1.0)
    currents = scatter_about(arg_keys[2], (2, SOURCES), 1.0, 6.0, ((1, 256),), jnp.float32)
    near_blocks = scatter_about(arg_keys[3], (NEAR_ALL, 2, ROW_DEV, STILE), 0.05, 0.3, ((0, 256),), jnp.float32)
    near_dest_keys = jax.random.split(jax.random.fold_in(arg_keys[4], 1), NEAR_ALL // NEAR_DEV)
    near_dest_turns = jax.random.permutation(jax.random.fold_in(arg_keys[4], 3), NEAR_ALL // NEAR_DEV)
    near_dest = jax.vmap(lambda own, number: deal_out(jax.random.fold_in(arg_keys[4], 2), own, number, NEAR_DEV, N_COL, 1, CAP, 2))(near_dest_keys, near_dest_turns).reshape((NEAR_ALL, 1))
    near_tile = place_ends(jax.random.randint(arg_keys[5], (NEAR_ALL, 1), 0, TILES), jax.random.fold_in(arg_keys[5], 1), 0, TILES - 1).astype(jnp.int32)
    return dict(test_points=test_points, src_points=src_points, currents=currents, near_blocks=near_blocks, near_dest=near_dest, near_tile=near_tile)


WAVENUMBER = 40.0
SOFTENING = 0.01

def kernel_sum(targets, sources, current):
    delta_x = targets[0][:, None] - sources[0][None, :]
    delta_y = targets[1][:, None] - sources[1][None, :]
    delta_z = targets[2][:, None] - sources[2][None, :]
    distance = jnp.sqrt(delta_x * delta_x + delta_y * delta_y + delta_z * delta_z + SOFTENING * SOFTENING)
    phases = WAVENUMBER * distance
    kernel_re = jnp.cos(phases) / distance
    kernel_im = -jnp.sin(phases) / distance
    real_part = lax.optimization_barrier(jnp.sum(kernel_re * current[0][None, :] - kernel_im * current[1][None, :], axis=1))
    imag_part = lax.optimization_barrier(jnp.sum(kernel_re * current[1][None, :] + kernel_im * current[0][None, :], axis=1))
    return jnp.stack([real_part, imag_part])

def reference(test_points, src_points, currents, near_blocks, near_dest, near_tile):
    block_rows = math.gcd(ROWS, 64)
    row_blocks = test_points.reshape(3, ROWS // block_rows, block_rows).transpose(1, 0, 2)
    far_blocks = lax.map(lambda targets: kernel_sum(targets, src_points, currents), row_blocks)
    far = far_blocks.transpose(1, 0, 2).reshape(2, ROWS)
    holder = (jnp.arange(NEAR_ALL) // NEAR_DEV).astype(jnp.int32)
    target = (holder // N_COL * N_COL + near_dest[:, 0]).astype(jnp.int32)
    tiled = currents.reshape(2, DEVICES, TILES, STILE)
    chosen = tiled[:, holder, near_tile[:, 0], :]
    highest = lax.Precision.HIGHEST
    term_re = jnp.einsum('kij,kj->ki', near_blocks[:, 0], chosen[0], precision=highest) - jnp.einsum('kij,kj->ki', near_blocks[:, 1], chosen[1], precision=highest)
    term_im = jnp.einsum('kij,kj->ki', near_blocks[:, 0], chosen[1], precision=highest) + jnp.einsum('kij,kj->ki', near_blocks[:, 1], chosen[0], precision=highest)
    terms = jnp.stack([term_re, term_im], axis=1)
    summed = jax.ops.segment_sum(terms, target, num_segments=DEVICES)
    near = summed.transpose(1, 0, 2).reshape(2, ROWS)
    return far * (1.0 / math.sqrt(SOURCES)) + near
```

```python
import functools
import math

import jax
import jax.numpy as jnp
from jax import lax
from jax.experimental import pallas as pl
from jax.experimental.pallas import tpu as pltpu
from jax.sharding import PartitionSpec as P

F32, BF16 = jnp.float32, jnp.bfloat16
MESH = pl.DeviceIdType.MESH
WAVENUMBER = 40.0
SOFTENING = 0.01
TURNS = WAVENUMBER / (2.0 * math.pi)
EPS2 = (TURNS * SOFTENING) ** 2
S0, S1, S2, S3 = 3.141557035259913, -5.166470369169727, 2.537091227972406, -0.544489261808413
B0, B1, B2 = S0 / S3, S1 / S3, S2 / S3
ONE = (1.0 + 4e-7) / S3**2
CHUNK = 128
LANES = 128
FEATURES = 80
ATAN = (0.9999998864, -0.3333259702, 0.1998590671, -0.1416122883, 0.1049894485, -0.07234855029, 0.03978119812, -0.01440134322, 0.002456721093)


def two(x):
    scaled = x * 65537.0
    high = scaled - (scaled - x)
    return high, x - high


def rows(base, *pairs):
    index = lax.broadcasted_iota(jnp.int32, base.shape, 0)
    for row, value in pairs:
        base = jnp.where(index == row, value, base)
    return base


def pieces(points, extra):
    coarse = jnp.round(points * 32.0) * (1.0 / 32.0)
    rest = points - coarse
    middle, rest2 = two(rest)
    fine, _ = two(rest2)
    grid = jnp.sum(coarse * coarse, axis=0, keepdims=True)
    off = jnp.sum(rest * (points + coarse), axis=0, keepdims=True) + extra
    g1, g2 = two(grid)
    o1, left = two(off)
    o2, o3 = two(left)
    return coarse, middle, fine, g1, g2, o1, o2, o3


def source_features(packed):
    points = rows(packed, *[(r, 0.0) for r in range(3, 8)])
    coarse, middle, fine, g1, g2, o1, o2, o3 = pieces(points, EPS2)
    a1, left = two(packed[4:5])
    a2, a3 = two(left)
    w1, left = two(packed[3:4])
    w2, w3 = two(left)
    zero = jnp.zeros_like(coarse)
    return [
        rows(coarse, (3, g1), (4, g2), (5, 1.0), (6, 1.0)),
        rows(coarse, (3, o1), (4, o2), (5, o3), (6, 1.0), (7, 1.0)),
        rows(coarse, (3, 1.0)),
        middle,
        fine,
        middle,
        middle,
        fine,
        rows(zero, (0, a1), (1, a2), (2, a3), (3, w1), (4, w2), (5, w3)),
        zero,
    ]


def target_features(points):
    coarse, middle, fine, g1, g2, o1, o2, o3 = pieces(points, 0.0)
    coarse, middle, fine = -2.0 * coarse, -2.0 * middle, -2.0 * fine
    zero = jnp.zeros_like(coarse)
    return [
        rows(coarse, (3, 1.0), (4, 1.0), (5, g1), (6, g2)),
        rows(middle, (3, 1.0), (4, 1.0), (5, 1.0), (6, o1), (7, o2)),
        rows(fine, (3, o3)),
        coarse,
        coarse,
        middle,
        fine,
        middle,
        zero,
        zero,
    ]


def pair_sums(q, shift, weight, sums):
    total, cosines, sines = sums
    inverse = lax.rsqrt(q)
    turns = q * inverse - shift
    part = turns - jnp.round(turns)
    z = part * part
    sine = part * (((z + B2) * z + B1) * z + B0)
    rest = ONE - sine * sine
    w = weight * inverse
    g = w * rest
    return total + w, cosines + g, sines + g * (sine * lax.rsqrt(rest))


def polar(re, im):
    are, aim = jnp.abs(re), jnp.abs(im)
    big, small = jnp.maximum(are, aim), jnp.minimum(are, aim)
    ratio = small / jnp.where(big > 0.0, big, 1.0)
    square = ratio * ratio
    angle = ATAN[-1]
    for c in ATAN[-2::-1]:
        angle = angle * square + c
    angle = angle * ratio * (0.5 / math.pi)
    angle = jnp.where(aim > are, 0.25 - angle, angle)
    angle = jnp.where(re < 0.0, 0.5 - angle, angle)
    return big * jnp.sqrt(1.0 + square), jnp.where(im < 0.0, -angle, angle)


def dot(a, b, ca, cb):
    return lax.dot_general(a.astype(BF16), b.astype(BF16), (((ca,), (cb,)), ((), ())), preferred_element_type=F32)


def near_rows(currents, blocks, dest, tile, planes):
    items, _, width, depth = blocks.shape
    tiles = currents.shape[1] // depth
    cur = jnp.concatenate(
        [currents[c : c + 1, t * depth : (t + 1) * depth] for c in range(2) for t in range(tiles)], axis=0
    )
    ch, cl = two(cur)
    both = jnp.concatenate([ch, cl], axis=0)
    n = items * width

    def against(part):
        bh, bl = two(blocks[:, part].reshape(n, depth))
        high = dot(both, bh, 1, 1)
        return high[: 2 * tiles] + high[2 * tiles :] + dot(ch, bl, 1, 1)

    ur, ui = against(0), against(1)
    real = ur[:tiles] - ui[tiles:]
    imag = ur[tiles:] + ui[:tiles]
    spread = (
        lax.broadcasted_iota(jnp.int32, (items, n), 1) // width == lax.broadcasted_iota(jnp.int32, (items, n), 0)
    ).astype(F32)
    along = lambda v, k: dot(jnp.broadcast_to(v.astype(F32), (items, k)), spread, 0, 0)
    mine = along(tile, tiles) == lax.broadcasted_iota(jnp.int32, (tiles, n), 0).astype(F32)
    real = jnp.sum(jnp.where(mine, real, 0.0), axis=0, keepdims=True)
    imag = jnp.sum(jnp.where(mine, imag, 0.0), axis=0, keepdims=True)
    plane = along(dest % planes, planes) == lax.broadcasted_iota(jnp.int32, (planes, n), 0).astype(F32)
    left = jnp.concatenate([jnp.where(plane, real, 0.0), jnp.where(plane, imag, 0.0)], axis=0)
    place = dot(spread, jnp.broadcast_to((dest // planes).astype(F32), (items, LANES)), 0, 0)
    lane = lax.broadcasted_iota(jnp.int32, (n, LANES), 1)
    row = lax.broadcasted_iota(jnp.int32, (n, LANES), 0)
    right = jnp.where((lane % width == row % width) & (place == (lane // width).astype(F32)), 1.0, 0.0)
    l1, rest = two(left)
    l2, l3 = two(rest)
    k = 2 * planes
    out = dot(jnp.concatenate([l1, l2, l3], axis=0), right, 1, 0)
    return out[:k] + out[k : 2 * k] + out[2 * k :]


def kernel(
    n_row, n_col, planes, scale,
    tp_ref, src_ref, cur_ref, blocks_hbm, dest_ref, tile_ref, out_ref,
    tbuf, sbuf, nbuf, nsend, rbuf, rsend, blocks, fa, fb, q_ref,
    copy_sem, tsend_sem, trecv_sem, ssend_sem, srecv_sem, nsend_sem, nrecv_sem, rsend_sem, rrecv_sem,
):
    places = n_col // planes
    members = n_row * places
    width = tp_ref.shape[1]
    n_src = src_ref.shape[1]
    n_tgt = n_row * LANES
    row, col = lax.axis_index("row"), lax.axis_index("col")
    place, plane = col // planes, col % planes
    me = row * places + place

    fetch = pltpu.make_async_copy(blocks_hbm, blocks, copy_sem)
    fetch.start()

    def member(k):
        other = lax.rem(me + k, members)
        return other, (other // places, lax.rem(other, places) * planes + plane)

    def level(k):
        other = lax.rem(plane + k, planes)
        return other, (row, place * planes + other)

    barrier = pltpu.get_barrier_semaphore()

    def greet(k, _):
        pl.semaphore_signal(barrier, inc=1, device_id=member(k)[1], device_id_type=MESH)
        return 0

    def greet_level(k, _):
        pl.semaphore_signal(barrier, inc=1, device_id=level(k)[1], device_id_type=MESH)
        return 0

    lax.fori_loop(1, planes, greet_level, 0)
    lax.fori_loop(1, members, greet, 0)

    points = (tp_ref[...] - 0.5) * TURNS
    repeated = jnp.concatenate([points] * (LANES // width), axis=1)
    lane = lax.broadcasted_iota(jnp.int32, repeated.shape, 1)
    tbuf[me] = jnp.concatenate(
        [jnp.where(lane // width == place, repeated, 0.0), jnp.zeros((1, LANES), F32)], axis=0
    )
    size, angle = polar(cur_ref[0:1, :], cur_ref[1:2, :])
    sbuf[plane] = jnp.concatenate(
        [(src_ref[...] - 0.5) * TURNS, size, angle, jnp.zeros((3, n_src), F32)], axis=0
    )

    for i in range(FEATURES // 8):
        fb[pl.ds(i * 8, 8), :] = jnp.zeros((8, n_tgt + 2 * LANES), BF16)
    index = lax.broadcasted_iota(jnp.int32, (16, LANES), 0)
    fb[pl.ds(64, 16), pl.ds(n_tgt, LANES)] = jnp.where(index < 3, 1.0, 0.0).astype(BF16)
    fb[pl.ds(64, 16), pl.ds(n_tgt + LANES, LANES)] = jnp.where((index >= 3) & (index < 6), 1.0, 0.0).astype(BF16)

    def prepare(which, slot):
        groups = source_features(sbuf[which])
        for i in range(0, len(groups), 2):
            fa[slot, pl.ds(i * 8, 16), :] = jnp.concatenate(groups[i : i + 2], axis=0).astype(BF16)

    prepare(plane, 0)

    fetch.wait()
    near = near_rows(cur_ref[...], blocks, dest_ref[...], tile_ref[...], planes)
    for k in range(planes):
        nsend[k] = jnp.concatenate([near[k : k + 1], near[planes + k : planes + k + 1]], axis=0)

    pl.semaphore_wait(barrier, members - 1 + planes - 1)

    def target_copy(k):
        other, device = member(k)
        return other, lambda slot, sem: pltpu.make_async_remote_copy(
            src_ref=tbuf.at[slot], dst_ref=tbuf.at[slot], send_sem=tsend_sem.at[other],
            recv_sem=trecv_sem.at[sem], device_id=device, device_id_type=MESH,
        )

    def source_copy(k):
        other, device = level(k)
        return other, lambda slot, sem: pltpu.make_async_remote_copy(
            src_ref=sbuf.at[slot], dst_ref=sbuf.at[slot], send_sem=ssend_sem.at[other],
            recv_sem=srecv_sem.at[sem], device_id=device, device_id_type=MESH,
        )

    def near_copy(k):
        other, device = level(k)
        return other, lambda slot, sem: pltpu.make_async_remote_copy(
            src_ref=nsend.at[other], dst_ref=nbuf.at[slot], send_sem=nsend_sem.at[other],
            recv_sem=nrecv_sem.at[sem], device_id=device, device_id_type=MESH,
        )

    def result_copy(k):
        other, device = member(k)
        return other, lambda slot, sem: pltpu.make_async_remote_copy(
            src_ref=rsend.at[other // places], dst_ref=rbuf.at[slot], send_sem=rsend_sem.at[other],
            recv_sem=rrecv_sem.at[sem], device_id=device, device_id_type=MESH,
        )

    def each(copy, count, mine, act):
        def body(k, _):
            other, make = copy(k)
            if act == "start":
                make(mine, mine).start()
            elif act == "recv":
                make(other, other).wait_recv()
            else:
                make(mine, mine).wait_send()
            return 0

        lax.fori_loop(1, count, body, 0)

    def offset(i):
        half = (i + 1) // 2
        return lax.rem(planes + (2 * lax.rem(i, 2) - 1) * half, planes)

    each(target_copy, members, me, "start")

    def send_source(i, _):
        _, make = source_copy(offset(i))
        make(plane, plane).start()
        return 0

    lax.fori_loop(1, planes, send_source, 0)
    nbuf[plane] = nsend[plane]
    each(near_copy, planes, plane, "start")

    each(target_copy, members, me, "recv")
    points = []
    for g in range(n_row):
        joined = tbuf[g * places]
        for s in range(1, places):
            joined = joined + tbuf[g * places + s]
        points.append(joined)
    points = jnp.concatenate(points, axis=1)
    points = jnp.concatenate([points, jnp.zeros((4, n_tgt), F32)], axis=0)
    groups = target_features(points)
    for i in range(0, len(groups), 2):
        fb[pl.ds(i * 8, 16), pl.ds(0, n_tgt)] = jnp.concatenate(groups[i : i + 2], axis=0).astype(BF16)

    chunks = n_src // CHUNK

    def distances(slot, chunk, into):
        part = fa[slot, :, pl.ds(chunk * CHUNK, CHUNK)]
        q_ref[into] = lax.dot_general(part, fb[...], (((0,), (0,)), ((), ())), preferred_element_type=F32)

    def add_up(chunk, sums):
        for r in range(CHUNK // 8):
            q = q_ref[chunk, pl.ds(r * 8, 8), pl.ds(0, n_tgt)]
            shift = q_ref[chunk, pl.ds(r * 8, 8), pl.ds(n_tgt, LANES)]
            weight = q_ref[chunk, pl.ds(r * 8, 8), pl.ds(n_tgt + LANES, LANES)]
            sums = pair_sums(q, jnp.tile(shift, (1, n_row)), jnp.tile(weight, (1, n_row)), sums)
        return sums

    distances(0, 0, 0)

    def block(i, sums):
        ahead = jnp.minimum(i + 1, planes - 1)

        @pl.when(i < planes - 1)
        def _():
            other, make = source_copy(offset(ahead))
            make(other, other).wait_recv()

        slot = lax.rem(i, 2)
        prepare(lax.rem(plane + offset(ahead), planes), 1 - slot)
        for c in range(chunks):
            if c < chunks - 1:
                distances(slot, c + 1, c + 1)
            else:
                distances(1 - slot, 0, 0)
            sums = add_up(c, sums)
        return sums

    zero = jnp.zeros((8, n_tgt), F32)
    total, cosines, sines = lax.fori_loop(0, planes, block, (zero, zero, zero))
    unit = scale * TURNS
    real = jnp.sum((2.0 * S3 * S3) * cosines - total, axis=0, keepdims=True) * unit
    imag = jnp.sum(sines, axis=0, keepdims=True) * (-2.0 * S3 * abs(S3) * unit)

    each(near_copy, planes, plane, "recv")
    near = nbuf[0]
    for k in range(1, planes):
        near = near + nbuf[k]
    for g in range(n_row):
        part = jnp.concatenate([real[:, g * LANES : (g + 1) * LANES], imag[:, g * LANES : (g + 1) * LANES]], axis=0)
        part = part + jnp.where(row == g, 1.0, 0.0) * near
        rsend[g] = part
    rbuf[me] = rsend[row]
    each(result_copy, members, me, "start")
    each(target_copy, members, me, "send")
    each(source_copy, planes, plane, "send")
    each(near_copy, planes, plane, "send")
    each(result_copy, members, me, "recv")
    field = rbuf[0]
    for k in range(1, members):
        field = field + rbuf[k]
    field = jnp.concatenate([field, jnp.zeros((6, LANES), F32)], axis=0)
    field = pltpu.roll(field, lax.rem(LANES - place * width, LANES), 1)
    out_ref[...] = field[0:2, 0:width]
    each(result_copy, members, me, "send")


def local(planes, total_sources, test_points, src_points, currents, near_blocks, near_dest, near_tile):
    n_row, n_col = lax.axis_size("row"), lax.axis_size("col")
    members = n_row * (n_col // planes)
    n_src = src_points.shape[1]
    n_tgt = n_row * LANES
    vmem = pl.BlockSpec(memory_space=pltpu.VMEM)
    dma = pltpu.SemaphoreType.DMA
    return pl.pallas_call(
        functools.partial(kernel, n_row, n_col, planes, 1.0 / math.sqrt(total_sources)),
        out_shape=jax.ShapeDtypeStruct((2, test_points.shape[1]), F32),
        in_specs=[vmem, vmem, vmem, pl.BlockSpec(memory_space=pl.ANY), vmem, vmem],
        out_specs=vmem,
        scratch_shapes=[
            pltpu.VMEM((members, 4, LANES), F32),
            pltpu.VMEM((planes, 8, n_src), F32),
            pltpu.VMEM((planes, 2, LANES), F32),
            pltpu.VMEM((planes, 2, LANES), F32),
            pltpu.VMEM((members, 2, LANES), F32),
            pltpu.VMEM((n_row, 2, LANES), F32),
            pltpu.VMEM(near_blocks.shape, F32),
            pltpu.VMEM((2, FEATURES, n_src), BF16),
            pltpu.VMEM((FEATURES, n_tgt + 2 * LANES), BF16),
            pltpu.VMEM((n_src // CHUNK, CHUNK, n_tgt + 2 * LANES), F32),
            dma,
            dma((members,)),
            dma((members,)),
            dma((planes,)),
            dma((planes,)),
            dma((planes,)),
            dma((planes,)),
            dma((members,)),
            dma((members,)),
        ],
        compiler_params=pltpu.CompilerParams(collective_id=0, has_side_effects=True, vmem_limit_bytes=48 << 20),
    )(test_points, src_points, currents, near_blocks, near_dest, near_tile)


def solution(mesh):
    planes = min(8, mesh.shape["col"])

    def whole(test_points, src_points, currents, near_blocks, near_dest, near_tile):
        both = ("row", "col")
        return jax.shard_map(
            functools.partial(local, planes, src_points.shape[1]),
            mesh=mesh,
            in_specs=(
                P(None, both), P(None, both), P(None, both), P(both, None, None, None), P(both, None), P(both, None),
            ),
            out_specs=P(None, both),
            check_vma=False,
        )(test_points, src_points, currents, near_blocks, near_dest, near_tile)

    return whole
```

```python
import functools
import math

import jax
import jax.numpy as jnp
from jax import lax
from jax.experimental import pallas as pl
from jax.experimental.pallas import tpu as pltpu
from jax.sharding import PartitionSpec as P

F32, BF16 = jnp.float32, jnp.bfloat16
MESH = pl.DeviceIdType.MESH
WAVENUMBER = 40.0
SOFTENING = 0.01
TURNS = WAVENUMBER / (2.0 * math.pi)
EPS2 = (TURNS * SOFTENING) ** 2
S0, S1, S2, S3 = 3.141557035259913, -5.166470369169727, 2.537091227972406, -0.544489261808413
B0, B1, B2 = S0 / S3, S1 / S3, S2 / S3
ONE = (1.0 + 4e-7) / S3**2
CHUNK = 128
LANES = 128
FEATURES = 80
ATAN = (0.9999998864, -0.3333259702, 0.1998590671, -0.1416122883, 0.1049894485, -0.07234855029, 0.03978119812, -0.01440134322, 0.002456721093)


def two(x):
    scaled = x * 65537.0
    high = scaled - (scaled - x)
    return high, x - high


def rows(base, *pairs):
    index = lax.broadcasted_iota(jnp.int32, base.shape, 0)
    for row, value in pairs:
        base = jnp.where(index == row, value, base)
    return base


def pieces(points, extra):
    coarse = jnp.round(points * 32.0) * (1.0 / 32.0)
    rest = points - coarse
    middle, rest2 = two(rest)
    fine, _ = two(rest2)
    grid = jnp.sum(coarse * coarse, axis=0, keepdims=True)
    off = jnp.sum(rest * (points + coarse), axis=0, keepdims=True) + extra
    g1, g2 = two(grid)
    o1, left = two(off)
    o2, o3 = two(left)
    return coarse, middle, fine, g1, g2, o1, o2, o3


def source_features(packed):
    points = rows(packed, *[(r, 0.0) for r in range(3, 8)])
    coarse, middle, fine, g1, g2, o1, o2, o3 = pieces(points, EPS2)
    a1, left = two(packed[4:5])
    a2, a3 = two(left)
    w1, left = two(packed[3:4])
    w2, w3 = two(left)
    zero = jnp.zeros_like(coarse)
    return [
        rows(coarse, (3, g1), (4, g2), (5, 1.0), (6, 1.0)),
        rows(coarse, (3, o1), (4, o2), (5, o3), (6, 1.0), (7, 1.0)),
        rows(coarse, (3, 1.0)),
        middle,
        fine,
        middle,
        middle,
        fine,
        rows(zero, (0, a1), (1, a2), (2, a3), (3, w1), (4, w2), (5, w3)),
        zero,
    ]


def target_features(points):
    coarse, middle, fine, g1, g2, o1, o2, o3 = pieces(points, 0.0)
    coarse, middle, fine = -2.0 * coarse, -2.0 * middle, -2.0 * fine
    zero = jnp.zeros_like(coarse)
    return [
        rows(coarse, (3, 1.0), (4, 1.0), (5, g1), (6, g2)),
        rows(middle, (3, 1.0), (4, 1.0), (5, 1.0), (6, o1), (7, o2)),
        rows(fine, (3, o3)),
        coarse,
        coarse,
        middle,
        fine,
        middle,
        zero,
        zero,
    ]


def pair_sums(q, shift, weight, sums):
    total, cosines, sines = sums
    inverse = lax.rsqrt(q)
    turns = q * inverse - shift
    part = turns - jnp.round(turns)
    z = part * part
    sine = part * (((z + B2) * z + B1) * z + B0)
    rest = ONE - sine * sine
    w = weight * inverse
    g = w * rest
    return total + w, cosines + g, sines + g * (sine * lax.rsqrt(rest))


def polar(re, im):
    are, aim = jnp.abs(re), jnp.abs(im)
    big, small = jnp.maximum(are, aim), jnp.minimum(are, aim)
    ratio = small / jnp.where(big > 0.0, big, 1.0)
    square = ratio * ratio
    angle = ATAN[-1]
    for c in ATAN[-2::-1]:
        angle = angle * square + c
    angle = angle * ratio * (0.5 / math.pi)
    angle = jnp.where(aim > are, 0.25 - angle, angle)
    angle = jnp.where(re < 0.0, 0.5 - angle, angle)
    return big * jnp.sqrt(1.0 + square), jnp.where(im < 0.0, -angle, angle)


def dot(a, b, ca, cb):
    return lax.dot_general(a.astype(BF16), b.astype(BF16), (((ca,), (cb,)), ((), ())), preferred_element_type=F32)


def near_rows(currents, blocks, dest, tile, planes):
    items, _, width, depth = blocks.shape
    tiles = currents.shape[1] // depth
    cur = jnp.concatenate(
        [currents[c : c + 1, t * depth : (t + 1) * depth] for c in range(2) for t in range(tiles)], axis=0
    )
    ch, cl = two(cur)
    both = jnp.concatenate([ch, cl], axis=0)
    n = items * width

    def against(part):
        bh, bl = two(blocks[:, part].reshape(n, depth))
        high = dot(both, bh, 1, 1)
        return high[: 2 * tiles] + high[2 * tiles :] + dot(ch, bl, 1, 1)

    ur, ui = against(0), against(1)
    real = ur[:tiles] - ui[tiles:]
    imag = ur[tiles:] + ui[:tiles]
    spread = (
        lax.broadcasted_iota(jnp.int32, (items, n), 1) // width == lax.broadcasted_iota(jnp.int32, (items, n), 0)
    ).astype(F32)
    along = lambda v, k: dot(jnp.broadcast_to(v.astype(F32), (items, k)), spread, 0, 0)
    mine = along(tile, tiles) == lax.broadcasted_iota(jnp.int32, (tiles, n), 0).astype(F32)
    real = jnp.sum(jnp.where(mine, real, 0.0), axis=0, keepdims=True)
    imag = jnp.sum(jnp.where(mine, imag, 0.0), axis=0, keepdims=True)
    plane = along(dest % planes, planes) == lax.broadcasted_iota(jnp.int32, (planes, n), 0).astype(F32)
    left = jnp.concatenate([jnp.where(plane, real, 0.0), jnp.where(plane, imag, 0.0)], axis=0)
    place = dot(spread, jnp.broadcast_to((dest // planes).astype(F32), (items, LANES)), 0, 0)
    lane = lax.broadcasted_iota(jnp.int32, (n, LANES), 1)
    row = lax.broadcasted_iota(jnp.int32, (n, LANES), 0)
    right = jnp.where((lane % width == row % width) & (place == (lane // width).astype(F32)), 1.0, 0.0)
    l1, rest = two(left)
    l2, l3 = two(rest)
    k = 2 * planes
    out = dot(jnp.concatenate([l1, l2, l3], axis=0), right, 1, 0)
    return out[:k] + out[k : 2 * k] + out[2 * k :]


def kernel(
    n_row, n_col, planes, scale,
    tp_ref, src_ref, cur_ref, blocks_hbm, dest_ref, tile_ref, out_ref,
    tbuf, sbuf, nbuf, nsend, rbuf, rsend, blocks, fa, fb, q_ref,
    copy_sem, tsend_sem, trecv_sem, ssend_sem, srecv_sem, nsend_sem, nrecv_sem, rsend_sem, rrecv_sem,
):
    places = n_col // planes
    members = n_row * places
    width = tp_ref.shape[1]
    n_src = src_ref.shape[1]
    n_tgt = n_row * LANES
    row, col = lax.axis_index("row"), lax.axis_index("col")
    place, plane = col // planes, col % planes
    me = row * places + place

    fetch = pltpu.make_async_copy(blocks_hbm, blocks, copy_sem)
    fetch.start()

    def member(k):
        other = lax.rem(me + k, members)
        return other, (other // places, lax.rem(other, places) * planes + plane)

    def level(k):
        other = lax.rem(plane + k, planes)
        return other, (row, place * planes + other)

    barrier = pltpu.get_barrier_semaphore()

    def greet(device):
        pl.semaphore_signal(barrier, inc=1, device_id=device, device_id_type=MESH)

    for k in range(1, members):
        greet(member(k)[1])
    for k in range(1, planes):
        greet(level(k)[1])

    points = (tp_ref[...] - 0.5) * TURNS
    repeated = jnp.concatenate([points] * (LANES // width), axis=1)
    lane = lax.broadcasted_iota(jnp.int32, repeated.shape, 1)
    tbuf[me] = jnp.concatenate(
        [jnp.where(lane // width == place, repeated, 0.0), jnp.zeros((1, LANES), F32)], axis=0
    )
    size, angle = polar(cur_ref[0:1, :], cur_ref[1:2, :])
    sbuf[plane] = jnp.concatenate(
        [(src_ref[...] - 0.5) * TURNS, size, angle, jnp.zeros((3, n_src), F32)], axis=0
    )

    for i in range(FEATURES // 8):
        fb[pl.ds(i * 8, 8), :] = jnp.zeros((8, n_tgt + 2 * LANES), BF16)
    index = lax.broadcasted_iota(jnp.int32, (16, LANES), 0)
    fb[pl.ds(64, 16), pl.ds(n_tgt, LANES)] = jnp.where(index < 3, 1.0, 0.0).astype(BF16)
    fb[pl.ds(64, 16), pl.ds(n_tgt + LANES, LANES)] = jnp.where((index >= 3) & (index < 6), 1.0, 0.0).astype(BF16)

    def prepare(which, slot):
        groups = source_features(sbuf[which])
        for i in range(0, len(groups), 2):
            fa[slot, pl.ds(i * 8, 16), :] = jnp.concatenate(groups[i : i + 2], axis=0).astype(BF16)

    prepare(plane, 0)

    pl.semaphore_wait(barrier, members - 1 + planes - 1)

    def target_copy(k):
        return pltpu.make_async_remote_copy(
            src_ref=tbuf.at[me], dst_ref=tbuf.at[me], send_sem=tsend_sem,
            recv_sem=trecv_sem, device_id=member(k)[1], device_id_type=MESH,
        )

    def source_copy(slot, device):
        return pltpu.make_async_remote_copy(
            src_ref=sbuf.at[slot], dst_ref=sbuf.at[slot], send_sem=ssend_sem,
            recv_sem=srecv_sem.at[slot], device_id=device, device_id_type=MESH,
        )

    def near_copy(k):
        other, device = level(k)
        return pltpu.make_async_remote_copy(
            src_ref=nsend.at[other], dst_ref=nbuf.at[plane], send_sem=nsend_sem,
            recv_sem=nrecv_sem, device_id=device, device_id_type=MESH,
        )

    def result_copy(k):
        other, device = member(k)
        return pltpu.make_async_remote_copy(
            src_ref=rsend.at[other // places], dst_ref=rbuf.at[me], send_sem=rsend_sem,
            recv_sem=rrecv_sem, device_id=device, device_id_type=MESH,
        )

    def all_of(buf, count, send_sem, recv_sem):
        part = buf.at[pl.ds(0, count)]
        return pltpu.make_async_remote_copy(
            src_ref=part, dst_ref=part, send_sem=send_sem,
            recv_sem=recv_sem, device_id=(row, col), device_id_type=MESH,
        )

    targets = all_of(tbuf, members - 1, tsend_sem, trecv_sem)
    nears = all_of(nbuf, planes - 1, nsend_sem, nrecv_sem)
    results = all_of(rbuf, members - 1, rsend_sem, rrecv_sem)
    sources = all_of(sbuf, planes - 1, ssend_sem, srecv_sem.at[0])

    def offset(i):
        half = (i + 1) // 2
        return lax.rem(planes + (2 * lax.rem(i, 2) - 1) * half, planes)

    for k in range(1, members):
        target_copy(k).start()

    def send_source(i, _):
        source_copy(plane, level(offset(i))[1]).start()
        return 0

    lax.fori_loop(1, planes, send_source, 0)

    fetch.wait()
    near = near_rows(cur_ref[...], blocks, dest_ref[...], tile_ref[...], planes)
    for k in range(planes):
        nsend[k] = jnp.concatenate([near[k : k + 1], near[planes + k : planes + k + 1]], axis=0)
    nbuf[plane] = nsend[plane]
    for k in range(1, planes):
        near_copy(k).start()

    targets.wait_recv()
    points = []
    for g in range(n_row):
        joined = tbuf[g * places]
        for s in range(1, places):
            joined = joined + tbuf[g * places + s]
        points.append(joined)
    points = jnp.concatenate(points, axis=1)
    points = jnp.concatenate([points, jnp.zeros((4, n_tgt), F32)], axis=0)
    groups = target_features(points)
    for i in range(0, len(groups), 2):
        fb[pl.ds(i * 8, 16), pl.ds(0, n_tgt)] = jnp.concatenate(groups[i : i + 2], axis=0).astype(BF16)

    chunks = n_src // CHUNK

    def distances(slot, chunk, into):
        part = fa[slot, :, pl.ds(chunk * CHUNK, CHUNK)]
        q_ref[into] = lax.dot_general(part, fb[...], (((0,), (0,)), ((), ())), preferred_element_type=F32)

    def add_up(chunk, sums):
        for r in range(CHUNK // 8):
            q = q_ref[chunk, pl.ds(r * 8, 8), pl.ds(0, n_tgt)]
            shift = q_ref[chunk, pl.ds(r * 8, 8), pl.ds(n_tgt, LANES)]
            weight = q_ref[chunk, pl.ds(r * 8, 8), pl.ds(n_tgt + LANES, LANES)]
            sums = pair_sums(q, jnp.tile(shift, (1, n_row)), jnp.tile(weight, (1, n_row)), sums)
        return sums

    distances(0, 0, 0)

    def block(i, sums):
        ahead = jnp.minimum(i + 1, planes - 1)

        @pl.when(i < planes - 1)
        def _():
            other, device = level(offset(ahead))
            source_copy(other, device).wait_recv()

        slot = lax.rem(i, 2)
        prepare(lax.rem(plane + offset(ahead), planes), 1 - slot)
        for c in range(chunks):
            if c < chunks - 1:
                distances(slot, c + 1, c + 1)
            else:
                distances(1 - slot, 0, 0)
            sums = add_up(c, sums)
        return sums

    zero = jnp.zeros((8, n_tgt), F32)
    total, cosines, sines = lax.fori_loop(0, planes, block, (zero, zero, zero))
    unit = scale * TURNS
    real = jnp.sum((2.0 * S3 * S3) * cosines - total, axis=0, keepdims=True) * unit
    imag = jnp.sum(sines, axis=0, keepdims=True) * (-2.0 * S3 * abs(S3) * unit)

    nears.wait_recv()
    near = nbuf[0]
    for k in range(1, planes):
        near = near + nbuf[k]
    for g in range(n_row):
        part = jnp.concatenate([real[:, g * LANES : (g + 1) * LANES], imag[:, g * LANES : (g + 1) * LANES]], axis=0)
        part = part + jnp.where(row == g, 1.0, 0.0) * near
        rsend[g] = part
    rbuf[me] = rsend[row]
    for k in range(1, members):
        result_copy(k).start()
    targets.wait_send()
    sources.wait_send()
    nears.wait_send()
    results.wait_recv()
    field = rbuf[0]
    for k in range(1, members):
        field = field + rbuf[k]
    field = jnp.concatenate([field, jnp.zeros((6, LANES), F32)], axis=0)
    field = pltpu.roll(field, lax.rem(LANES - place * width, LANES), 1)
    out_ref[...] = field[0:2, 0:width]
    results.wait_send()


def local(planes, total_sources, test_points, src_points, currents, near_blocks, near_dest, near_tile):
    n_row, n_col = lax.axis_size("row"), lax.axis_size("col")
    members = n_row * (n_col // planes)
    n_src = src_points.shape[1]
    n_tgt = n_row * LANES
    vmem = pl.BlockSpec(memory_space=pltpu.VMEM)
    dma = pltpu.SemaphoreType.DMA
    return pl.pallas_call(
        functools.partial(kernel, n_row, n_col, planes, 1.0 / math.sqrt(total_sources)),
        out_shape=jax.ShapeDtypeStruct((2, test_points.shape[1]), F32),
        in_specs=[vmem, vmem, vmem, pl.BlockSpec(memory_space=pl.ANY), vmem, vmem],
        out_specs=vmem,
        scratch_shapes=[
            pltpu.VMEM((members, 4, LANES), F32),
            pltpu.VMEM((planes, 8, n_src), F32),
            pltpu.VMEM((planes, 2, LANES), F32),
            pltpu.VMEM((planes, 2, LANES), F32),
            pltpu.VMEM((members, 2, LANES), F32),
            pltpu.VMEM((n_row, 2, LANES), F32),
            pltpu.VMEM(near_blocks.shape, F32),
            pltpu.VMEM((2, FEATURES, n_src), BF16),
            pltpu.VMEM((FEATURES, n_tgt + 2 * LANES), BF16),
            pltpu.VMEM((n_src // CHUNK, CHUNK, n_tgt + 2 * LANES), F32),
            dma,
            dma,
            dma,
            dma,
            dma((planes,)),
            dma,
            dma,
            dma,
            dma,
        ],
        compiler_params=pltpu.CompilerParams(collective_id=0, has_side_effects=True, vmem_limit_bytes=48 << 20),
    )(test_points, src_points, currents, near_blocks, near_dest, near_tile)


def solution(mesh):
    planes = min(8, mesh.shape["col"])

    def whole(test_points, src_points, currents, near_blocks, near_dest, near_tile):
        both = ("row", "col")
        return jax.shard_map(
            functools.partial(local, planes, src_points.shape[1]),
            mesh=mesh,
            in_specs=(
                P(None, both), P(None, both), P(None, both), P(both, None, None, None), P(both, None), P(both, None),
            ),
            out_specs=P(None, both),
            check_vma=False,
        )(test_points, src_points, currents, near_blocks, near_dest, near_tile)

    return whole
```

```python
import functools
import math

import jax
import jax.numpy as jnp
from jax import lax
from jax.experimental import pallas as pl
from jax.experimental.pallas import tpu as pltpu
from jax.sharding import PartitionSpec as P

F32, BF16 = jnp.float32, jnp.bfloat16
MESH = pl.DeviceIdType.MESH
WAVENUMBER = 40.0
SOFTENING = 0.01
TURNS = WAVENUMBER / (2.0 * math.pi)
EPS2 = (TURNS * SOFTENING) ** 2
S0, S1, S2, S3 = 3.141557035259913, -5.166470369169727, 2.537091227972406, -0.544489261808413
B0, B1, B2 = S0 / S3, S1 / S3, S2 / S3
ONE = (1.0 + 4e-7) / S3**2
CHUNK = 128
LANES = 128
FEATURES = 80
ATAN = (0.9999998864, -0.3333259702, 0.1998590671, -0.1416122883, 0.1049894485, -0.07234855029, 0.03978119812, -0.01440134322, 0.002456721093)


def two(x):
    scaled = x * 65537.0
    high = scaled - (scaled - x)
    return high, x - high


def rows(base, *pairs):
    index = lax.broadcasted_iota(jnp.int32, base.shape, 0)
    for row, value in pairs:
        base = jnp.where(index == row, value, base)
    return base


def pieces(points, extra):
    coarse = jnp.round(points * 32.0) * (1.0 / 32.0)
    rest = points - coarse
    middle, rest2 = two(rest)
    fine, _ = two(rest2)
    grid = jnp.sum(coarse * coarse, axis=0, keepdims=True)
    off = jnp.sum(rest * (points + coarse), axis=0, keepdims=True) + extra
    g1, g2 = two(grid)
    o1, left = two(off)
    o2, o3 = two(left)
    return coarse, middle, fine, g1, g2, o1, o2, o3


def source_features(packed):
    points = rows(packed, *[(r, 0.0) for r in range(3, 8)])
    coarse, middle, fine, g1, g2, o1, o2, o3 = pieces(points, EPS2)
    a1, left = two(packed[4:5])
    a2, a3 = two(left)
    w1, left = two(packed[3:4])
    w2, w3 = two(left)
    zero = jnp.zeros_like(coarse)
    return [
        rows(coarse, (3, g1), (4, g2), (5, 1.0), (6, 1.0)),
        rows(coarse, (3, o1), (4, o2), (5, o3), (6, 1.0), (7, 1.0)),
        rows(coarse, (3, 1.0)),
        middle,
        fine,
        middle,
        middle,
        fine,
        rows(zero, (0, a1), (1, a2), (2, a3), (3, w1), (4, w2), (5, w3)),
        zero,
    ]


def target_features(points):
    coarse, middle, fine, g1, g2, o1, o2, o3 = pieces(points, 0.0)
    coarse, middle, fine = -2.0 * coarse, -2.0 * middle, -2.0 * fine
    zero = jnp.zeros_like(coarse)
    return [
        rows(coarse, (3, 1.0), (4, 1.0), (5, g1), (6, g2)),
        rows(middle, (3, 1.0), (4, 1.0), (5, 1.0), (6, o1), (7, o2)),
        rows(fine, (3, o3)),
        coarse,
        coarse,
        middle,
        fine,
        middle,
        zero,
        zero,
    ]


def pair_sums(q, shift, weight, sums):
    total, cosines, sines = sums
    inverse = lax.rsqrt(q)
    turns = q * inverse - shift
    part = turns - jnp.round(turns)
    z = part * part
    sine = part * (((z + B2) * z + B1) * z + B0)
    rest = ONE - sine * sine
    w = weight * inverse
    g = w * rest
    return total + w, cosines + g, sines + g * (sine * lax.rsqrt(rest))


def polar(re, im):
    are, aim = jnp.abs(re), jnp.abs(im)
    big, small = jnp.maximum(are, aim), jnp.minimum(are, aim)
    ratio = small / jnp.where(big > 0.0, big, 1.0)
    square = ratio * ratio
    angle = ATAN[-1]
    for c in ATAN[-2::-1]:
        angle = angle * square + c
    angle = angle * ratio * (0.5 / math.pi)
    angle = jnp.where(aim > are, 0.25 - angle, angle)
    angle = jnp.where(re < 0.0, 0.5 - angle, angle)
    return big * jnp.sqrt(1.0 + square), jnp.where(im < 0.0, -angle, angle)


def dot(a, b, ca, cb):
    return lax.dot_general(a.astype(BF16), b.astype(BF16), (((ca,), (cb,)), ((), ())), preferred_element_type=F32)


def near_rows(currents, blocks, dest, tile, planes):
    items, _, width, depth = blocks.shape
    tiles = currents.shape[1] // depth
    cur = jnp.concatenate(
        [currents[c : c + 1, t * depth : (t + 1) * depth] for c in range(2) for t in range(tiles)], axis=0
    )
    ch, cl = two(cur)
    both = jnp.concatenate([ch, cl], axis=0)
    n = items * width

    def against(part):
        bh, bl = two(blocks[:, part].reshape(n, depth))
        high = dot(both, bh, 1, 1)
        return high[: 2 * tiles] + high[2 * tiles :] + dot(ch, bl, 1, 1)

    ur, ui = against(0), against(1)
    real = ur[:tiles] - ui[tiles:]
    imag = ur[tiles:] + ui[:tiles]
    spread = (
        lax.broadcasted_iota(jnp.int32, (items, n), 1) // width == lax.broadcasted_iota(jnp.int32, (items, n), 0)
    ).astype(F32)
    along = lambda v, k: dot(jnp.broadcast_to(v.astype(F32), (k, items)), spread, 1, 0)
    mine = along(tile, tiles) == lax.broadcasted_iota(jnp.int32, (tiles, n), 0).astype(F32)
    real = jnp.sum(jnp.where(mine, real, 0.0), axis=0, keepdims=True)
    imag = jnp.sum(jnp.where(mine, imag, 0.0), axis=0, keepdims=True)
    plane = along(dest % planes, planes) == lax.broadcasted_iota(jnp.int32, (planes, n), 0).astype(F32)
    left = jnp.concatenate([jnp.where(plane, real, 0.0), jnp.where(plane, imag, 0.0)], axis=0)
    place = dot(spread, jnp.broadcast_to((dest // planes).astype(F32), (LANES, items)), 0, 1)
    lane = lax.broadcasted_iota(jnp.int32, (n, LANES), 1)
    row = lax.broadcasted_iota(jnp.int32, (n, LANES), 0)
    right = jnp.where((lane % width == row % width) & (place == (lane // width).astype(F32)), 1.0, 0.0)
    l1, rest = two(left)
    l2, l3 = two(rest)
    k = 2 * planes
    out = dot(jnp.concatenate([l1, l2, l3], axis=0), right, 1, 0)
    return out[:k] + out[k : 2 * k] + out[2 * k :]


def kernel(
    n_row, n_col, planes, scale,
    tp_hbm, src_hbm, cur_hbm, blocks_hbm, dest_hbm, tile_hbm, out_ref,
    tp_ref, src_ref, cur_ref, dest_ref, tile_ref, tbuf, sbuf, nbuf, nsend, rbuf, rsend, blocks, fa, fb, q_ref,
    copy_sem, tsend_sem, trecv_sem, ssend_sem, srecv_sem, nsend_sem, nrecv_sem, rsend_sem, rrecv_sem,
):
    places = n_col // planes
    members = n_row * places
    width = tp_ref.shape[1]
    n_src = src_ref.shape[1]
    n_tgt = n_row * LANES
    row, col = lax.axis_index("row"), lax.axis_index("col")
    place, plane = col // planes, col % planes
    me = row * places + place

    fetches = [
        pltpu.make_async_copy(a, b, copy_sem.at[i])
        for i, (a, b) in enumerate((
            (tp_hbm, tp_ref), (cur_hbm, cur_ref), (src_hbm, src_ref),
            (dest_hbm, dest_ref), (tile_hbm, tile_ref), (blocks_hbm, blocks),
        ))
    ]
    for fetch in fetches:
        fetch.start()

    def member(k):
        other = lax.rem(me + k, members)
        return other, (other // places, lax.rem(other, places) * planes + plane)

    def level(k):
        other = lax.rem(plane + k, planes)
        return other, (row, place * planes + other)

    barrier = pltpu.get_barrier_semaphore()

    def greet(device):
        pl.semaphore_signal(barrier, inc=1, device_id=device, device_id_type=MESH)

    for k in range(1, members):
        greet(member(k)[1])
    for k in range(1, planes):
        greet(level(k)[1])

    for i in range(FEATURES // 8):
        fb[pl.ds(i * 8, 8), :] = jnp.zeros((8, n_tgt + 2 * LANES), BF16)
    index = lax.broadcasted_iota(jnp.int32, (16, LANES), 0)
    fb[pl.ds(64, 16), pl.ds(n_tgt, LANES)] = jnp.where(index < 3, 1.0, 0.0).astype(BF16)
    fb[pl.ds(64, 16), pl.ds(n_tgt + LANES, LANES)] = jnp.where((index >= 3) & (index < 6), 1.0, 0.0).astype(BF16)

    for fetch in fetches[:3]:
        fetch.wait()

    points = (tp_ref[...] - 0.5) * TURNS
    repeated = jnp.concatenate([points] * (LANES // width), axis=1)
    lane = lax.broadcasted_iota(jnp.int32, repeated.shape, 1)
    tbuf[me] = jnp.concatenate(
        [jnp.where(lane // width == place, repeated, 0.0), jnp.zeros((1, LANES), F32)], axis=0
    )
    size, angle = polar(cur_ref[0:1, :], cur_ref[1:2, :])
    sbuf[plane] = jnp.concatenate(
        [(src_ref[...] - 0.5) * TURNS, size, angle, jnp.zeros((3, n_src), F32)], axis=0
    )

    def prepare(which, slot):
        groups = source_features(sbuf[which])
        for i in range(0, len(groups), 2):
            fa[slot, pl.ds(i * 8, 16), :] = jnp.concatenate(groups[i : i + 2], axis=0).astype(BF16)

    prepare(plane, 0)

    pl.semaphore_wait(barrier, members - 1 + planes - 1)

    def target_copy(k):
        return pltpu.make_async_remote_copy(
            src_ref=tbuf.at[me], dst_ref=tbuf.at[me], send_sem=tsend_sem,
            recv_sem=trecv_sem, device_id=member(k)[1], device_id_type=MESH,
        )

    def source_copy(slot, device):
        return pltpu.make_async_remote_copy(
            src_ref=sbuf.at[slot], dst_ref=sbuf.at[slot], send_sem=ssend_sem,
            recv_sem=srecv_sem.at[slot], device_id=device, device_id_type=MESH,
        )

    def near_copy(k):
        other, device = level(k)
        return pltpu.make_async_remote_copy(
            src_ref=nsend.at[other], dst_ref=nbuf.at[plane], send_sem=nsend_sem,
            recv_sem=nrecv_sem, device_id=device, device_id_type=MESH,
        )

    def result_copy(k):
        other, device = member(k)
        return pltpu.make_async_remote_copy(
            src_ref=rsend.at[other // places], dst_ref=rbuf.at[me], send_sem=rsend_sem,
            recv_sem=rrecv_sem, device_id=device, device_id_type=MESH,
        )

    def all_of(buf, count, send_sem, recv_sem):
        part = buf.at[pl.ds(0, count)]
        return pltpu.make_async_remote_copy(
            src_ref=part, dst_ref=part, send_sem=send_sem,
            recv_sem=recv_sem, device_id=(row, col), device_id_type=MESH,
        )

    targets = all_of(tbuf, members - 1, tsend_sem, trecv_sem)
    nears = all_of(nbuf, planes - 1, nsend_sem, nrecv_sem)
    results = all_of(rbuf, members - 1, rsend_sem, rrecv_sem)
    sources = all_of(sbuf, planes - 1, ssend_sem, srecv_sem.at[0])

    def offset(i):
        half = (i + 1) // 2
        return lax.rem(planes + (2 * lax.rem(i, 2) - 1) * half, planes)

    for k in range(1, members):
        target_copy(k).start()

    def send_source(i, _):
        source_copy(plane, level(offset(i))[1]).start()
        return 0

    lax.fori_loop(1, planes, send_source, 0)

    for fetch in fetches[3:]:
        fetch.wait()
    near = near_rows(cur_ref[...], blocks, dest_ref[...], tile_ref[...], planes)
    for k in range(planes):
        nsend[k] = jnp.concatenate([near[k : k + 1], near[planes + k : planes + k + 1]], axis=0)
    nbuf[plane] = nsend[plane]
    for k in range(1, planes):
        near_copy(k).start()

    targets.wait_recv()
    points = []
    for g in range(n_row):
        joined = tbuf[g * places]
        for s in range(1, places):
            joined = joined + tbuf[g * places + s]
        points.append(joined)
    points = jnp.concatenate(points, axis=1)
    points = jnp.concatenate([points, jnp.zeros((4, n_tgt), F32)], axis=0)
    groups = target_features(points)
    for i in range(0, len(groups), 2):
        fb[pl.ds(i * 8, 16), pl.ds(0, n_tgt)] = jnp.concatenate(groups[i : i + 2], axis=0).astype(BF16)

    chunks = n_src // CHUNK

    def distances(slot, chunk, into):
        part = fa[slot, :, pl.ds(chunk * CHUNK, CHUNK)]
        q_ref[into] = lax.dot_general(part, fb[...], (((0,), (0,)), ((), ())), preferred_element_type=F32)

    def add_up(chunk, sums):
        for r in range(CHUNK // 8):
            q = q_ref[chunk, pl.ds(r * 8, 8), pl.ds(0, n_tgt)]
            shift = q_ref[chunk, pl.ds(r * 8, 8), pl.ds(n_tgt, LANES)]
            weight = q_ref[chunk, pl.ds(r * 8, 8), pl.ds(n_tgt + LANES, LANES)]
            sums = pair_sums(q, jnp.tile(shift, (1, n_row)), jnp.tile(weight, (1, n_row)), sums)
        return sums

    distances(0, 0, 0)

    def block(i, sums):
        ahead = jnp.minimum(i + 1, planes - 1)

        @pl.when(i < planes - 1)
        def _():
            other, device = level(offset(ahead))
            source_copy(other, device).wait_recv()

        slot = lax.rem(i, 2)
        prepare(lax.rem(plane + offset(ahead), planes), 1 - slot)
        for c in range(chunks):
            if c < chunks - 1:
                distances(slot, c + 1, c + 1)
            else:
                distances(1 - slot, 0, 0)
            sums = add_up(c, sums)
        return sums

    zero = jnp.zeros((8, n_tgt), F32)
    total, cosines, sines = lax.fori_loop(0, planes, block, (zero, zero, zero))
    unit = scale * TURNS
    real = jnp.sum((2.0 * S3 * S3) * cosines - total, axis=0, keepdims=True) * unit
    imag = jnp.sum(sines, axis=0, keepdims=True) * (-2.0 * S3 * abs(S3) * unit)

    nears.wait_recv()
    near = nbuf[0]
    for k in range(1, planes):
        near = near + nbuf[k]
    for g in range(n_row):
        part = jnp.concatenate([real[:, g * LANES : (g + 1) * LANES], imag[:, g * LANES : (g + 1) * LANES]], axis=0)
        part = part + jnp.where(row == g, 1.0, 0.0) * near
        rsend[g] = part
    rbuf[me] = rsend[row]
    for k in range(1, members):
        result_copy(k).start()
    targets.wait_send()
    sources.wait_send()
    nears.wait_send()
    results.wait_recv()
    field = rbuf[0]
    for k in range(1, members):
        field = field + rbuf[k]
    field = jnp.concatenate([field, jnp.zeros((6, LANES), F32)], axis=0)
    field = pltpu.roll(field, lax.rem(LANES - place * width, LANES), 1)
    out_ref[...] = field[0:2, 0:width]
    results.wait_send()


def local(planes, total_sources, test_points, src_points, currents, near_blocks, near_dest, near_tile):
    n_row, n_col = lax.axis_size("row"), lax.axis_size("col")
    members = n_row * (n_col // planes)
    n_src = src_points.shape[1]
    n_tgt = n_row * LANES
    vmem = pl.BlockSpec(memory_space=pltpu.VMEM)
    dma = pltpu.SemaphoreType.DMA
    return pl.pallas_call(
        functools.partial(kernel, n_row, n_col, planes, 1.0 / math.sqrt(total_sources)),
        out_shape=jax.ShapeDtypeStruct((2, test_points.shape[1]), F32),
        in_specs=[pl.BlockSpec(memory_space=pltpu.HBM)] * 6,
        out_specs=vmem,
        scratch_shapes=[
            pltpu.VMEM(test_points.shape, F32),
            pltpu.VMEM(src_points.shape, F32),
            pltpu.VMEM(currents.shape, F32),
            pltpu.VMEM((1, near_dest.shape[0]), jnp.int32),
            pltpu.VMEM((1, near_tile.shape[0]), jnp.int32),
            pltpu.VMEM((members, 4, LANES), F32),
            pltpu.VMEM((planes, 8, n_src), F32),
            pltpu.VMEM((planes, 2, LANES), F32),
            pltpu.VMEM((planes, 2, LANES), F32),
            pltpu.VMEM((members, 2, LANES), F32),
            pltpu.VMEM((n_row, 2, LANES), F32),
            pltpu.VMEM(near_blocks.shape, F32),
            pltpu.VMEM((2, FEATURES, n_src), BF16),
            pltpu.VMEM((FEATURES, n_tgt + 2 * LANES), BF16),
            pltpu.VMEM((n_src // CHUNK, CHUNK, n_tgt + 2 * LANES), F32),
            dma((6,)),
            dma,
            dma,
            dma,
            dma((planes,)),
            dma,
            dma,
            dma,
            dma,
        ],
        compiler_params=pltpu.CompilerParams(collective_id=0, has_side_effects=True, vmem_limit_bytes=67_043_328),
    )(test_points, src_points, currents, near_blocks, near_dest.reshape(1, -1), near_tile.reshape(1, -1))


def solution(mesh):
    planes = min(8, mesh.shape["col"])

    def whole(test_points, src_points, currents, near_blocks, near_dest, near_tile):
        both = ("row", "col")
        return jax.shard_map(
            functools.partial(local, planes, src_points.shape[1]),
            mesh=mesh,
            in_specs=(
                P(None, both), P(None, both), P(None, both), P(both, None, None, None), P(both, None), P(both, None),
            ),
            out_specs=P(None, both),
            check_vma=False,
        )(test_points, src_points, currents, near_blocks, near_dest, near_tile)

    return whole
```
